256 devices in a mesh: wide: 32 (over y, x, core), narrow: 8 (over z).
Axes of the slice: x: 4, y: 4, z: 8, core: 2. Of those that a mesh axis runs over, the one named last changes fastest.
Arguments:
- amplitudes: bfloat16 [1024, 16, 4096], P('wide', None, 'narrow'), may hold values from -6 to 6
- amp_tiles: int32 [32, 16], replicated, may hold values from 0 to 31, all different within a row
- integrals: bfloat16 [32, 2, 4096, 4096], P('wide', None, None, 'narrow'), may hold values from -0.09375 to 0.09375
- cd_tiles: int32 [32, 2], replicated, may hold values from 0 to 31, all different within a row
- q_owner: int32 [32], replicated, may hold values from 0 to 31, each once
Outputs:
- residual: bfloat16 [1024, 32, 4096], P('wide', None, 'narrow')
The draws below stay inside these ranges and needn't reach their ends.
Inputs may be any that keep to these rules, and one draw needn't show every extreme that they name: `amp_tiles`: within a row, the 16 tiles are different. `cd_tiles`: within a row, the 2 tiles are different; every tile is named by some row. `q_owner`: each owner index appears once.
All inputs are finite; a program needn't handle non-finite values.
Results may differ from the reference program's by a relative error of at most 0.017.
Values may be sent and summed in bfloat16 or wider, within the bound.
A program may use at most 64 MiB of HBM per device.

```python
import jax
import jax.numpy as jnp
from jax import lax

KV = 2
PAIR = 4096
NS = 32
NBLK = 32
TW = 16
OCC_PAIRS = 1024
N_NARROW = 8


def shard_levels(rng, extent, shards, least, high):
    factor_of, own = 1.0, jax.random.fold_in(rng, 6)
    for axis_at, shards_of in shards:
        draws = jnp.exp(jax.random.uniform(jax.random.fold_in(own, axis_at), (shards_of,), jnp.float32, least / len(shards), high / len(shards)))
        factor_of = factor_of * jnp.repeat(draws, extent[axis_at] // shards_of).reshape([-1 if axis == axis_at else 1 for axis in range(len(extent))])
    return factor_of


def different_ones(stream_key, rows, amount, top, lift):
    sequence = jax.random.permutation(jax.random.fold_in(stream_key, 1), amount)
    favour = sequence
    for power in range(3):
        favour = favour * favour // amount
    favour = favour * lift // amount
    lots = jax.random.randint(jax.random.fold_in(stream_key, 2), (rows, amount), 0, 4096) + favour
    holders = jax.random.permutation(jax.random.fold_in(stream_key, 3), rows)[jnp.arange(amount) % rows]
    lots = jnp.where(jnp.arange(rows)[:, None] == holders[None, :], 1 << 14, lots)
    merit = lots * amount + jnp.arange(amount)
    return lax.top_k(merit.astype(jnp.int32), top)[1].astype(jnp.int32)


def centred(own_key, shape, width, limit, cuts=(), held_as=jnp.bfloat16):
    entries = jax.random.normal(own_key, shape, jnp.float32) * width
    if len(cuts) > 0:
        entries = shard_levels(own_key, shape, cuts, -0.22, 0.18) * entries
    return jnp.clip(entries, min=-limit, max=limit).astype(held_as)


def setup_inputs(seed: int = 0) -> dict:
    keys = jax.random.split(jax.random.key(seed), 6)
    amplitudes = centred(keys[0], (OCC_PAIRS, TW, PAIR), 1.0, 6.0, ((0, 32), (2, 8)))
    amp_tiles = different_ones(keys[1], NBLK, NS, TW, 8192)
    integrals = centred(keys[2], (NS, KV, PAIR, PAIR), (KV * PAIR // 2) ** -0.5, 0.09375, ((0, 32), (3, 8)))
    cd_tiles = different_ones(keys[3], NS, NS, KV, 0)
    q_owner = jax.random.permutation(keys[4], NS).astype(jnp.int32)
    return dict(amplitudes=amplitudes, amp_tiles=amp_tiles, integrals=integrals, cd_tiles=cd_tiles, q_owner=q_owner)


def reference(amplitudes, amp_tiles, integrals, cd_tiles, q_owner):
    nblk = amp_tiles.shape[0]
    rows_dev = amplitudes.shape[0] // nblk
    tile_width = amp_tiles.shape[1]
    block_amps = amplitudes.reshape(nblk, rows_dev, tile_width, PAIR).astype(jnp.float32)

    def one_tile(tile):
        owner_slot = q_owner[tile]
        tile_ints = integrals[owner_slot].astype(jnp.float32).reshape(KV, PAIR, N_NARROW, PAIR // N_NARROW)
        wanted = cd_tiles[tile]
        picker = (amp_tiles[:, :, None] == wanted[None, None, :]).astype(jnp.float32)
        chosen = jnp.einsum("btk,brtc->brkc", picker, block_amps, precision=lax.Precision.HIGHEST)
        chosen = chosen.reshape(nblk * rows_dev, KV, N_NARROW, PAIR // N_NARROW)
        parts = jnp.einsum("rkjc,kpjc->jrp", chosen, tile_ints, precision=lax.Precision.HIGHEST)
        rounded = lax.optimization_barrier(parts.astype(jnp.bfloat16)).astype(jnp.float32)
        return jnp.sum(rounded, axis=0).astype(jnp.bfloat16)

    stacked = lax.map(one_tile, jnp.arange(q_owner.shape[0], dtype=jnp.int32))
    return jnp.transpose(stacked, (1, 0, 2))
```

```python
import functools

import jax
import jax.numpy as jnp
from jax import lax
from jax.experimental import pallas as pl
from jax.experimental.pallas import tpu as pltpu
from jax.sharding import PartitionSpec as P

MESH = pl.DeviceIdType.MESH
F32, BF16, I32 = jnp.float32, jnp.bfloat16, jnp.int32

NB = 32
RB = 32
TW = 16
KV = 2
NZ = 8
W = 512
BPC = 4
NC = NB // BPC
R = BPC * RB
H = R // 2
SX, SY = 4, 4


def offset(slot):
    chip = slot // 2
    return chip // SX, chip % SX, slot % 2


def shifted(y, x, core, slot, sign):
    dy, dx, dc = offset(slot)
    if sign < 0:
        dy, dx = SY - dy, SX - dx
    return (lax.rem(y + dy, SY) * SX + lax.rem(x + dx, SX)) * 2 + lax.rem(core + dc, 2)


def dot(a, b):
    return lax.dot_general(a, b, (((1,), (0,)), ((), ())), preferred_element_type=F32)


def dot_t(a, b):
    return lax.dot_general(a, b, (((1,), (1,)), ((), ())), preferred_element_type=F32)


def kernel(
    amp_tiles, cd_tiles, q_owner, amp_hbm, ints_hbm, out_hbm,
    amp, ints, wanted, owner_rows, tile_lanes, amp_out, amp_in, first, right_in, left_in, fin_out, fin_in, out,
    load_sem, amp_send, amp_recv, right_send, right_recv, left_send, left_recv, fin_send, fin_recv,
):
    me = lax.axis_index("wide")
    z = lax.axis_index("narrow")
    core, x, y = lax.rem(me, 2), lax.rem(me // 2, SX), me // (2 * SX)
    z_right, z_left = lax.rem(z + 1, NZ), lax.rem(z + NZ - 1, NZ)

    load_amp = pltpu.make_async_copy(amp_hbm, amp, load_sem.at[0])
    load_ints = pltpu.make_async_copy(ints_hbm, ints, load_sem.at[1])
    load_amp.start()
    load_ints.start()

    barrier = pltpu.get_barrier_semaphore()
    for slot in range(1, NB):
        pl.semaphore_signal(barrier, inc=1, device_id=(shifted(y, x, core, slot, 1), z), device_id_type=MESH)
    for there in (z_right, z_left):
        pl.semaphore_signal(barrier, inc=1, device_id=(me, there), device_id_type=MESH)

    rows = lax.broadcasted_iota(I32, (NB, 128), 0)
    lanes = lax.broadcasted_iota(I32, (1, 128), 1)
    owners = jnp.zeros((NB, 128), I32)
    wants = [jnp.zeros((NB, 128), I32) for _ in range(KV)]
    for q in range(NB):
        owner = q_owner[q]
        owners = jnp.where(rows == q, owner, owners)
        for k in range(KV):
            wants[k] = jnp.where(rows == owner, cd_tiles[k, q], wants[k])
    owner_rows[...] = owners
    for k in range(KV):
        wanted[k] = wants[k]
    held = jnp.zeros((1, 128), I32)
    for t in range(TW):
        held = jnp.where(lax.rem(lanes, TW) == t, amp_tiles[t, me], held)
    tile_lanes[...] = jnp.broadcast_to(held, (8, 128))

    def amp_copy(slot):
        return pltpu.make_async_remote_copy(
            src_ref=amp_out.at[slot], dst_ref=amp_in.at[slot], send_sem=amp_send.at[slot], recv_sem=amp_recv.at[slot],
            device_id=(shifted(y, x, core, slot, 1), z), device_id_type=MESH)

    def fin_copy(slot):
        return pltpu.make_async_remote_copy(
            src_ref=fin_out.at[slot], dst_ref=fin_in.at[slot], send_sem=fin_send.at[slot], recv_sem=fin_recv.at[slot],
            device_id=(shifted(y, x, core, slot, -1), z), device_id_type=MESH)

    def right_copy(step, chunk):
        if step == 0:
            src, dst = first.at[chunk, pl.ds(0, H)], right_in.at[0, chunk, pl.ds(0, H)]
        else:
            src, dst = right_in.at[step - 1, chunk], right_in.at[step, chunk]
        return pltpu.make_async_remote_copy(
            src_ref=src, dst_ref=dst, send_sem=right_send.at[step, chunk], recv_sem=right_recv.at[step, chunk],
            device_id=(me, z_right), device_id_type=MESH)

    def left_copy(step, chunk):
        if step == 0:
            src, dst = first.at[chunk, pl.ds(H, H)], left_in.at[0, chunk, pl.ds(H, H)]
        else:
            src, dst = left_in.at[step - 1, chunk], left_in.at[step, chunk]
        return pltpu.make_async_remote_copy(
            src_ref=src, dst_ref=dst, send_sem=left_send.at[step, chunk], recv_sem=left_recv.at[step, chunk],
            device_id=(me, z_left), device_id_type=MESH)

    load_amp.wait()
    pl.semaphore_wait(barrier, NB - 1 + 2)

    spread_rows = lax.broadcasted_iota(I32, (RB, RB * TW), 0)
    spread_lanes = lax.broadcasted_iota(I32, (RB, RB * TW), 1)
    spread = jnp.where(spread_lanes // TW == spread_rows, 1.0, 0.0)

    @pl.loop(0, NC)
    def _(chunk):
        pieces = []
        for u in range(BPC):
            there = shifted(y, x, core, chunk * BPC + u, 1)
            for k in range(KV):
                hit = jnp.where(tile_lanes[pl.ds(0, 1), :] == wanted[k, pl.ds(there, 1), :], 1.0, 0.0)
                hit = jnp.concatenate([hit] * (RB * TW // 128), axis=1)
                pieces.append((spread * hit).astype(BF16))
        picked = dot(jnp.concatenate(pieces, axis=0), amp[...]).astype(BF16)
        amp_out[pl.ds(chunk * BPC, BPC)] = picked.reshape(BPC, KV, RB, W)

        @pl.when(chunk == 0)
        def _():
            amp_in[0] = picked[: KV * RB].reshape(KV, RB, W)

        for u in range(BPC):
            @pl.when(chunk * BPC + u > 0)
            def _():
                amp_copy(chunk * BPC + u).start()

    load_ints.wait()

    def term(chunk, part):
        total = None
        for k in range(KV):
            left = amp_in[pl.ds(chunk * BPC, BPC), k].reshape(R, W)
            value = dot_t(left, ints[k, part])
            total = value if total is None else total + value
        return total

    @pl.loop(0, NC + 5)
    def _(t):
        @pl.when(t < NC)
        def _():
            for u in range(BPC):
                @pl.when(t * BPC + u > 0)
                def _():
                    amp_copy(t * BPC + u).wait_recv()
            first[t] = term(t, lax.rem(z + 4, NZ)).astype(BF16)
            right_copy(0, t).start()
            left_copy(0, t).start()

        for step in range(1, 4):
            chunk = t - step

            @pl.when((chunk >= 0) & (chunk < NC))
            def _():
                value = term(chunk, lax.rem(z + 4 - step, NZ))
                right_copy(step - 1, chunk).wait_recv()
                if step == 1:
                    right_in[0, chunk, :H] = (value[:H] + right_in[0, chunk, :H].astype(F32)).astype(BF16)
                    right_in[0, chunk, H:] = value[H:].astype(BF16)
                else:
                    right_in[step - 1, chunk] = (value + right_in[step - 1, chunk].astype(F32)).astype(BF16)
                right_copy(step, chunk).start()
                value = term(chunk, lax.rem(z + NZ - 4 + step, NZ))
                left_copy(step - 1, chunk).wait_recv()
                if step == 1:
                    left_in[0, chunk, :H] = value[:H].astype(BF16)
                    left_in[0, chunk, H:] = (value[H:] + left_in[0, chunk, H:].astype(F32)).astype(BF16)
                else:
                    left_in[step - 1, chunk] = (value + left_in[step - 1, chunk].astype(F32)).astype(BF16)
                left_copy(step, chunk).start()

        last = t - 4

        @pl.when((last >= 0) & (last < NC))
        def _():
            value = term(last, z)
            right_copy(3, last).wait_recv()
            left_copy(3, last).wait_recv()
            value = value + right_in[3, last].astype(F32) + left_in[3, last].astype(F32)
            done = value.astype(BF16).reshape(BPC, RB, W)
            fin_out[pl.ds(last * BPC, BPC)] = done

            @pl.when(last == 0)
            def _():
                fin_in[0] = done[0]

            for u in range(BPC):
                @pl.when(last * BPC + u > 0)
                def _():
                    fin_copy(last * BPC + u).start()

        back = t - 5

        @pl.when(back >= 0)
        def _():
            source = jnp.zeros((1, 128), I32)
            for u in range(BPC):
                source = jnp.where(lanes // RB == u, shifted(y, x, core, back * BPC + u, 1), source)
            match = jnp.where(owner_rows[...] == source, 1.0, 0.0)
            for u in range(BPC):
                @pl.when(back * BPC + u > 0)
                def _():
                    fin_copy(back * BPC + u).wait_recv()
            values = fin_in[pl.ds(back * BPC, BPC)].reshape(R, W)
            for r in range(0, RB, 4):
                place = jnp.concatenate([jnp.where(lax.rem(lanes, RB) == r + i, match, 0.0) for i in range(4)], axis=0)
                moved = dot(place.astype(BF16), values)
                span = pl.ds(r * NB, 4 * NB)

                @pl.when(back == 0)
                def _():
                    out[span, :] = moved.astype(BF16)

                @pl.when(back > 0)
                def _():
                    out[span, :] = (moved + out[span, :].astype(F32)).astype(BF16)

    store = pltpu.make_async_copy(out, out_hbm, load_sem.at[2])
    store.start()

    @pl.loop(1, NB)
    def _(slot):
        amp_copy(slot).wait_send()
        fin_copy(slot).wait_send()

    @pl.loop(0, NC)
    def _(chunk):
        for step in range(4):
            right_copy(step, chunk).wait_send()
            left_copy(step, chunk).wait_send()

    store.wait()


def on_device(amplitudes, amp_tiles, integrals, cd_tiles, q_owner):
    any_space = pl.BlockSpec(memory_space=pl.ANY)
    smem = pl.BlockSpec(memory_space=pltpu.SMEM)
    dma = pltpu.SemaphoreType.DMA
    result = pl.pallas_call(
        kernel,
        out_shape=jax.ShapeDtypeStruct((RB * NB, W), BF16),
        in_specs=[smem, smem, smem, any_space, any_space],
        out_specs=any_space,
        scratch_shapes=[
            pltpu.VMEM((RB * TW, W), BF16),
            pltpu.VMEM((KV, NZ, W, W), BF16),
            pltpu.VMEM((KV, NB, 128), I32),
            pltpu.VMEM((NB, 128), I32),
            pltpu.VMEM((8, 128), I32),
            pltpu.VMEM((NB, KV, RB, W), BF16),
            pltpu.VMEM((NB, KV, RB, W), BF16),
            pltpu.VMEM((NC, R, W), BF16),
            pltpu.VMEM((4, NC, R, W), BF16),
            pltpu.VMEM((4, NC, R, W), BF16),
            pltpu.VMEM((NB, RB, W), BF16),
            pltpu.VMEM((NB, RB, W), BF16),
            pltpu.VMEM((RB * NB, W), BF16),
            dma((3,)), dma((NB,)), dma((NB,)),
            dma((4, NC)), dma((4, NC)), dma((4, NC)), dma((4, NC)),
            dma((NB,)), dma((NB,)),
        ],
        compiler_params=pltpu.CompilerParams(
            collective_id=0, has_side_effects=True, vmem_limit_bytes=56 * 1024 * 1024),
        name="ladder",
    )(amp_tiles.T, cd_tiles.T, q_owner, amplitudes.reshape(RB * TW, W), integrals.reshape(KV, NZ, W, W))
    return result.reshape(RB, NB, W)


def solution(mesh):
    placed = (P("wide", None, "narrow"), P(), P("wide", None, None, "narrow"), P(), P())
    return jax.shard_map(
        on_device, mesh=mesh, in_specs=placed, out_specs=P("wide", None, "narrow"), check_vma=False
    )
```

```python
import jax
import jax.numpy as jnp
from jax import lax
from jax.experimental import pallas as pl
from jax.experimental.pallas import tpu as pltpu
from jax.sharding import PartitionSpec as P

MESH = pl.DeviceIdType.MESH
F32, BF16, I32 = jnp.float32, jnp.bfloat16, jnp.int32

NB = 32
RB = 32
TW = 16
KV = 2
NZ = 8
W = 512
SX, SY = 4, 4
CHIPS = [(0, 1), (0, 3), (1, 0), (1, 1), (3, 3), (1, 3), (3, 1), (0, 2), (2, 0), (2, 1), (2, 3), (1, 2), (3, 2), (2, 2), (3, 0)]
NC = len(CHIPS) + 2
AHEAD = 4


def digits(values):
    code = sum(v << (2 * i) for i, v in enumerate(values))
    return code - (1 << 32) if code >= 1 << 31 else code


DY, DX = digits([0] + [c[0] for c in CHIPS]), digits([0] + [c[1] for c in CHIPS])


def offset(slot):
    if isinstance(slot, int):
        return (*((0, 0) if slot in (0, NB - 1) else CHIPS[(slot - 1) // 2]), (slot + 1) % 2 if 0 < slot < NB - 1 else slot % 2)
    at = 2 * lax.rem((slot + 1) // 2, 16)
    last = slot // (NB - 1)
    core = jnp.where(slot == 0, 0, lax.rem(slot + 1 + last, 2))
    return lax.shift_right_logical(jnp.int32(DY), at) & 3, lax.shift_right_logical(jnp.int32(DX), at) & 3, core


def shifted(y, x, core, slot, sign):
    dy, dx, dc = offset(slot)
    if sign < 0:
        dy, dx = SY - dy, SX - dx
    return (lax.rem(y + dy, SY) * SX + lax.rem(x + dx, SX)) * 2 + lax.rem(core + dc, 2)


def by_size(chunk, run):
    edge = (chunk == 0) | (chunk == NC - 1)

    @pl.when(edge)
    def _():
        run(chunk // (NC - 1) * (NB - 1), 1)

    @pl.when((chunk > 0) & (chunk < NC - 1))
    def _():
        run(2 * chunk - 1, 2)


def rows_of(slot, blocks):
    return pl.ds(pl.multiple_of(slot * RB, RB), blocks * RB)


def halves_of(slot, blocks):
    half = blocks * RB // 2
    start = pl.multiple_of(slot * RB, RB)
    return pl.ds(start, half), pl.ds(pl.multiple_of(start + half, 16), half)


def dot(a, b):
    return lax.dot_general(a, b, (((1,), (0,)), ((), ())), preferred_element_type=F32)


def dot_t(a, b):
    return lax.dot_general(a, b, (((1,), (1,)), ((), ())), preferred_element_type=F32)


def kernel(
    amp_tiles, cd_tiles, q_owner, amp_hbm, ints_hbm, out,
    amp, ints, wanted, tile_lanes, amp_out, amp_in, first, right_in, left_in, fin_out,
    load_sem, ints_sem, amp_send, amp_recv, right_send, right_recv, left_send, left_recv, fin_send, fin_recv,
):
    me = lax.axis_index("wide")
    z = lax.axis_index("narrow")
    core, x, y = lax.rem(me, 2), lax.rem(me // 2, SX), me // (2 * SX)
    z_right, z_left = lax.rem(z + 1, NZ), lax.rem(z + NZ - 1, NZ)

    def ints_copy(part):
        return pltpu.make_async_copy(ints_hbm.at[:, part], ints.at[:, part], ints_sem.at[part])

    load_amp = pltpu.make_async_copy(amp_hbm, amp, load_sem.at[0])
    load_amp.start()
    ints_copy(lax.rem(z + 4, NZ)).start()

    barrier = pltpu.get_barrier_semaphore()
    for slot in range(1, NB):
        pl.semaphore_signal(barrier, inc=1, device_id=(shifted(y, x, core, slot, 1), z), device_id_type=MESH)
    for there in (z_right, z_left):
        pl.semaphore_signal(barrier, inc=1, device_id=(me, there), device_id_type=MESH)

    rows = lax.broadcasted_iota(I32, (NB, 128), 0)
    lanes = lax.broadcasted_iota(I32, (1, 128), 1)
    wants = [jnp.zeros((NB, 128), I32) for _ in range(KV)]
    for q in range(NB):
        owner = q_owner[q]
        for k in range(KV):
            wants[k] = jnp.where(rows == owner, cd_tiles[k, q], wants[k])
    for k in range(KV):
        wanted[k] = wants[k]
    held = jnp.zeros((1, 128), I32)
    for t in range(TW):
        held = jnp.where(lax.rem(lanes, TW) == t, amp_tiles[t, me], held)
    tile_lanes[...] = jnp.broadcast_to(held, (8, 128))
    for distance in (3, 5, 2, 6, 1, 7, 0):
        ints_copy(lax.rem(z + distance, NZ)).start()

    def amp_copy(slot):
        return pltpu.make_async_remote_copy(
            src_ref=amp_out.at[slot], dst_ref=amp_in.at[slot], send_sem=amp_send.at[slot], recv_sem=amp_recv.at[slot],
            device_id=(shifted(y, x, core, slot, 1), z), device_id_type=MESH)

    def fin_copy(slot):
        return pltpu.make_async_remote_copy(
            src_ref=fin_out.at[rows_of(slot, 1)], dst_ref=out.at[me], send_sem=fin_send.at[slot],
            recv_sem=fin_recv.at[slot], device_id=(shifted(y, x, core, slot, -1), z), device_id_type=MESH)

    def ring_copy(held, sends, recvs, there, side, step, chunk, slot, blocks):
        if step == 0:
            span = halves_of(slot, blocks)[side]
            src, dst = first.at[span], held.at[0, span]
        else:
            span = rows_of(slot, blocks)
            src, dst = held.at[step - 1, span], held.at[step, span]
        return pltpu.make_async_remote_copy(
            src_ref=src, dst_ref=dst, send_sem=sends.at[step, chunk], recv_sem=recvs.at[step, chunk],
            device_id=(me, there), device_id_type=MESH)

    def right_copy(*where):
        return ring_copy(right_in, right_send, right_recv, z_right, 0, *where)

    def left_copy(*where):
        return ring_copy(left_in, left_send, left_recv, z_left, 1, *where)

    own_rows = pltpu.make_async_copy(fin_out.at[pl.ds(0, RB)], out.at[me], load_sem.at[1])
    load_amp.wait()

    spread_rows = lax.broadcasted_iota(I32, (RB, RB * TW), 0)
    spread_lanes = lax.broadcasted_iota(I32, (RB, RB * TW), 1)
    spread = jnp.where(spread_lanes // TW == spread_rows, 1.0, 0.0)

    def pick(slot, blocks):
        pieces = []
        for u in range(blocks):
            there = shifted(y, x, core, slot + u, 1)
            for k in range(KV):
                hit = jnp.where(tile_lanes[pl.ds(0, 1), :] == wanted[k, pl.ds(there, 1), :], 1.0, 0.0)
                hit = jnp.concatenate([hit] * (RB * TW // 128), axis=1)
                pieces.append((spread * hit).astype(BF16))
        picked = dot(jnp.concatenate(pieces, axis=0), amp[...]).astype(BF16)
        return picked.reshape(blocks, KV, RB, W)

    def send_amplitudes(slot, blocks):
        amp_out[pl.ds(slot, blocks)] = pick(slot, blocks)
        for u in range(blocks):
            amp_copy(slot + u).start()

    amp_in[0] = pick(0, 1)[0]
    pl.semaphore_wait(barrier, NB - 1 + 2)

    @pl.loop(1, AHEAD)
    def _(chunk):
        send_amplitudes(2 * chunk - 1, 2)

    def term(slot, blocks, part):
        total = None
        for k in range(KV):
            left = amp_in[pl.ds(slot, blocks), k].reshape(blocks * RB, W)
            value = dot_t(left, ints[k, part])
            total = value if total is None else total + value
        return total

    @pl.loop(0, NC + 4)
    def _(t):
        def start(slot, blocks):
            for u in range(blocks):
                @pl.when(slot + u > 0)
                def _():
                    amp_copy(slot + u).wait_recv()

            if blocks == 1:
                @pl.when(slot == 0)
                def _():
                    ints_copy(lax.rem(z + 4, NZ)).wait()
            first[rows_of(slot, blocks), :] = term(slot, blocks, lax.rem(z + 4, NZ)).astype(BF16)
            right_copy(0, t, slot, blocks).start()
            left_copy(0, t, slot, blocks).start()

        @pl.when(t < NC)
        def _():
            by_size(t, start)

        @pl.when(2 * t < NC - 1 - AHEAD)
        def _():
            send_amplitudes(2 * (AHEAD + 2 * t) - 1, 2)

        @pl.when(2 * t + 1 < NC - 1 - AHEAD)
        def _():
            send_amplitudes(2 * (AHEAD + 2 * t) + 1, 2)

        @pl.when(2 * t == NC - 1 - AHEAD + (NC - 1 - AHEAD) % 2)
        def _():
            send_amplitudes(NB - 1, 1)

        for step in range(1, 4):
            chunk = t - step

            def move(slot, blocks):
                if blocks == 1:
                    @pl.when(slot == 0)
                    def _():
                        ints_copy(lax.rem(z + 4 - step, NZ)).wait()
                        ints_copy(lax.rem(z + NZ - 4 + step, NZ)).wait()

                everything = rows_of(slot, blocks)
                half = blocks * RB // 2
                spans = halves_of(slot, blocks)
                for side, (held, copy, part) in enumerate((
                    (right_in, right_copy, lax.rem(z + 4 - step, NZ)),
                    (left_in, left_copy, lax.rem(z + NZ - 4 + step, NZ)),
                )):
                    value = term(slot, blocks, part)
                    copy(step - 1, chunk, slot, blocks).wait_recv()
                    if step == 1:
                        came, new = spans[side], spans[1 - side]
                        parts = (value[:half], value[half:])
                        held[0, came, :] = (parts[side] + held[0, came, :].astype(F32)).astype(BF16)
                        held[0, new, :] = parts[1 - side].astype(BF16)
                    else:
                        held[step - 1, everything, :] = (value + held[step - 1, everything, :].astype(F32)).astype(BF16)
                    copy(step, chunk, slot, blocks).start()

            @pl.when((chunk >= 0) & (chunk < NC))
            def _():
                by_size(chunk, move)

        last = t - 4

        def finish(slot, blocks):
            if blocks == 1:
                @pl.when(slot == 0)
                def _():
                    ints_copy(z).wait()

            everything = rows_of(slot, blocks)
            value = term(slot, blocks, z)
            right_copy(3, last, slot, blocks).wait_recv()
            left_copy(3, last, slot, blocks).wait_recv()
            value = value + right_in[3, everything, :].astype(F32) + left_in[3, everything, :].astype(F32)
            fin_out[everything, :] = value.astype(BF16)
            if blocks == 1:
                @pl.when(slot == 0)
                def _():
                    own_rows.start()
            for u in range(blocks):
                @pl.when(slot + u > 0)
                def _():
                    fin_copy(slot + u).start()

        @pl.when(last >= 0)
        def _():
            by_size(last, finish)

    own_rows.wait()

    @pl.loop(1, NB)
    def _(slot):
        amp_copy(slot).wait_send()
        fin_copy(slot).wait()

    @pl.loop(0, NC)
    def _(chunk):
        def drain(slot, blocks):
            for step in range(4):
                right_copy(step, chunk, slot, blocks).wait_send()
                left_copy(step, chunk, slot, blocks).wait_send()

        by_size(chunk, drain)


def on_device(amplitudes, amp_tiles, integrals, cd_tiles, q_owner):
    any_space = pl.BlockSpec(memory_space=pl.ANY)
    smem = pl.BlockSpec(memory_space=pltpu.SMEM)
    dma = pltpu.SemaphoreType.DMA
    result = pl.pallas_call(
        kernel,
        out_shape=jax.ShapeDtypeStruct((NB, RB, W), BF16),
        in_specs=[smem, smem, smem, any_space, any_space],
        out_specs=any_space,
        scratch_shapes=[
            pltpu.VMEM((RB * TW, W), BF16),
            pltpu.VMEM((KV, NZ, W, W), BF16),
            pltpu.VMEM((KV, NB, 128), I32),
            pltpu.VMEM((8, 128), I32),
            pltpu.VMEM((NB, KV, RB, W), BF16),
            pltpu.VMEM((NB, KV, RB, W), BF16),
            pltpu.VMEM((NB * RB, W), BF16),
            pltpu.VMEM((4, NB * RB, W), BF16),
            pltpu.VMEM((4, NB * RB, W), BF16),
            pltpu.VMEM((NB * RB, W), BF16),
            dma((2,)), dma((NZ,)), dma((NB,)), dma((NB,)),
            dma((4, NC)), dma((4, NC)), dma((4, NC)), dma((4, NC)),
            dma((NB,)), dma((NB,)),
        ],
        compiler_params=pltpu.CompilerParams(
            collective_id=0, has_side_effects=True, vmem_limit_bytes=56 * 1024 * 1024),
        name="ladder",
    )(amp_tiles.T, cd_tiles.T, q_owner, amplitudes.reshape(RB * TW, W), integrals.reshape(KV, NZ, W, W))
    return jnp.transpose(jnp.take(result, q_owner, axis=0, mode="clip"), (1, 0, 2))


def solution(mesh):
    placed = (P("wide", None, "narrow"), P(), P("wide", None, None, "narrow"), P(), P())
    return jax.shard_map(
        on_device, mesh=mesh, in_specs=placed, out_specs=P("wide", None, "narrow"), check_vma=False
    )
```

```python
import functools

import jax
import jax.numpy as jnp
from jax import lax
from jax.experimental import pallas as pl
from jax.experimental.pallas import tpu as pltpu
from jax.sharding import PartitionSpec as P

MESH = pl.DeviceIdType.MESH
F32, BF16, I32 = jnp.float32, jnp.bfloat16, jnp.int32

NB = 32
RB = 32
TW = 16
KV = 2
NZ = 8
W = 512
BPC = 2
NC = NB // BPC
R = BPC * RB
H = R // 2
PW = 256
STRIDE = 40
SX, SY = 4, 4
AHEAD = 4
SINGLE = 2
CHIPS = [(0, 0), (0, 1), (0, 3), (1, 0), (1, 1), (3, 3), (1, 3), (3, 1), (0, 2), (2, 0), (2, 1), (2, 3), (1, 2), (3, 2), (2, 2), (3, 0)]


def digits(values):
    code = sum(v << (2 * i) for i, v in enumerate(values))
    return code - (1 << 32) if code >= 1 << 31 else code


DY, DX = digits([c[0] for c in CHIPS]), digits([c[1] for c in CHIPS])


def offset(slot):
    chip = slot // 2
    if isinstance(slot, int):
        return (*CHIPS[chip], slot % 2)
    at = 2 * chip
    return lax.shift_right_logical(jnp.int32(DY), at) & 3, lax.shift_right_logical(jnp.int32(DX), at) & 3, slot % 2


def shifted(y, x, core, slot, sign):
    dy, dx, dc = offset(slot)
    if sign < 0:
        dy, dx = SY - dy, SX - dx
    return (lax.rem(y + dy, SY) * SX + lax.rem(x + dx, SX)) * 2 + lax.rem(core + dc, 2)


def dot(a, b):
    return lax.dot_general(a, b, (((1,), (0,)), ((), ())), preferred_element_type=F32)


def dot_t(a, b):
    return lax.dot_general(a, b, (((1,), (1,)), ((), ())), preferred_element_type=F32)


def kernel(
    tiles_hbm, cd_hbm, owner_hbm, amp_hbm, ints_hbm, out,
    amp_tiles, cd_tiles, q_owner,
    amp, ints, wanted, tile_lanes, amp_out, amp_in, first, own, right_in, left_in, fin_out,
    load_sem, ints_sem, amp_send, amp_recv, right_send, right_recv, left_send, left_recv, fin_send, fin_recv,
):
    me = lax.axis_index("wide")
    z = lax.axis_index("narrow")
    core, x, y = lax.rem(me, 2), lax.rem(me // 2, SX), me // (2 * SX)
    z_right, z_left = lax.rem(z + 1, NZ), lax.rem(z + NZ - 1, NZ)

    def ints_copy(part):
        return pltpu.make_async_copy(ints_hbm.at[:, part], ints.at[:, part], ints_sem.at[part])

    load_amp = pltpu.make_async_copy(amp_hbm, amp, load_sem.at[0])
    load_tables = [
        pltpu.make_async_copy(src, dst, load_sem.at[2 + i])
        for i, (src, dst) in enumerate(((tiles_hbm, amp_tiles), (cd_hbm, cd_tiles), (owner_hbm, q_owner)))
    ]
    for load in load_tables:
        load.start()
    load_amp.start()
    ints_copy(lax.rem(z + 4, NZ)).start()

    barrier = pltpu.get_barrier_semaphore()
    for slot in range(1, NB):
        pl.semaphore_signal(barrier, inc=1, device_id=(shifted(y, x, core, slot, 1), z), device_id_type=MESH)
    for there in (z_right, z_left):
        pl.semaphore_signal(barrier, inc=1, device_id=(me, there), device_id_type=MESH)

    for load in load_tables:
        load.wait()
    rows = lax.broadcasted_iota(I32, (NB, 128), 0)
    lanes = lax.broadcasted_iota(I32, (1, 128), 1)
    wants = [jnp.zeros((NB, 128), I32) for _ in range(KV)]
    for q in range(NB):
        owner = q_owner[q]
        for k in range(KV):
            wants[k] = jnp.where(rows == owner, cd_tiles[k, q], wants[k])
    for k in range(KV):
        wanted[k] = wants[k]
    held = jnp.zeros((1, 128), I32)
    for t in range(TW):
        held = jnp.where(lax.rem(lanes, TW) == t, amp_tiles[t, me], held)
    tile_lanes[...] = jnp.broadcast_to(held, (8, 128))

    def amp_copy(slot):
        return pltpu.make_async_remote_copy(
            src_ref=amp_out.at[slot], dst_ref=amp_in.at[slot], send_sem=amp_send.at[slot], recv_sem=amp_recv.at[slot],
            device_id=(shifted(y, x, core, slot, 1), z), device_id_type=MESH)

    def fin_copy(slot):
        return pltpu.make_async_remote_copy(
            src_ref=fin_out.at[slot], dst_ref=out.at[me], send_sem=fin_send.at[slot], recv_sem=fin_recv.at[slot],
            device_id=(shifted(y, x, core, slot, -1), z), device_id_type=MESH)

    def right_copy(step, chunk):
        if step == 0:
            src, dst = first.at[chunk, pl.ds(0, H)], right_in.at[0, chunk, pl.ds(0, H)]
        else:
            src, dst = right_in.at[step - 1, chunk], right_in.at[step, chunk]
        return pltpu.make_async_remote_copy(
            src_ref=src, dst_ref=dst, send_sem=right_send.at[step, chunk], recv_sem=right_recv.at[step, chunk],
            device_id=(me, z_right), device_id_type=MESH)

    def left_copy(step, chunk):
        if step == 0:
            src, dst = first.at[chunk, pl.ds(H, H)], left_in.at[0, chunk, pl.ds(H, H)]
        else:
            src, dst = left_in.at[step - 1, chunk], left_in.at[step, chunk]
        return pltpu.make_async_remote_copy(
            src_ref=src, dst_ref=dst, send_sem=left_send.at[step, chunk], recv_sem=left_recv.at[step, chunk],
            device_id=(me, z_left), device_id_type=MESH)

    for distance in (3, 5, 2, 6, 1, 7, 0):
        ints_copy(lax.rem(z + distance, NZ)).start()

    own_rows = pltpu.make_async_copy(fin_out.at[0], out.at[me], load_sem.at[1])
    load_amp.wait()
    pl.semaphore_wait(barrier, NB - 1 + 2)

    spread_rows = lax.broadcasted_iota(I32, (RB, RB * TW), 0)
    spread_lanes = lax.broadcasted_iota(I32, (RB, RB * TW), 1)
    spread = jnp.where(spread_lanes // TW == spread_rows, 1.0, 0.0)

    def send_amplitudes(chunk):
        pieces = []
        for u in range(BPC):
            there = shifted(y, x, core, chunk * BPC + u, 1)
            for k in range(KV):
                hit = jnp.where(tile_lanes[pl.ds(0, 1), :] == wanted[k, pl.ds(there, 1), :], 1.0, 0.0)
                hit = jnp.concatenate([hit] * (RB * TW // 128), axis=1)
                pieces.append((spread * hit).astype(BF16))
        picked = dot(jnp.concatenate(pieces, axis=0), amp[...]).astype(BF16)
        amp_out[pl.ds(chunk * BPC, BPC)] = picked.reshape(BPC, KV, RB, W)

        @pl.when(chunk == 0)
        def _():
            amp_in[0] = picked[: KV * RB].reshape(KV, RB, W)

        for u in range(BPC):
            @pl.when(chunk * BPC + u > 0)
            def _():
                amp_copy(chunk * BPC + u).start()

    @pl.loop(0, AHEAD)
    def _(chunk):
        send_amplitudes(chunk)

    def multiply(chunk, part, store):
        def go(amount):
            total = None
            for k in range(KV):
                left = amp_in[pl.ds(chunk * BPC, amount * BPC), k].reshape(amount * R, W)
                value = dot_t(left, ints[k, part])
                total = value if total is None else total + value
            store(pl.ds(chunk, amount), total.reshape(amount, R, W))

        @pl.when(chunk == 0)
        def _():
            ints_copy(part).wait()

        @pl.when(chunk < SINGLE)
        def _():
            go(1)

        @pl.when((chunk >= SINGLE) & (chunk % 2 == 0))
        def _():
            go(2)

    def keep(index):
        def store(span, value):
            own[index, span] = value

        return store

    def keep_first(span, value):
        first[span] = value.astype(BF16)

    def arrived(chunk):
        for u in range(BPC):
            @pl.when(chunk * BPC + u > 0)
            def _():
                amp_copy(chunk * BPC + u).wait_recv()

    @pl.loop(0, NC + 4)
    def _(t):
        @pl.when(t < NC)
        def _():
            @pl.when((t < SINGLE) | (t % 2 == 0))
            def _():
                arrived(t)

            @pl.when((t >= SINGLE) & (t % 2 == 0))
            def _():
                arrived(t + 1)

            multiply(t, lax.rem(z + 4, NZ), keep_first)
            right_copy(0, t).start()
            left_copy(0, t).start()

        for step in (1, 2, 3):
            chunk = t - step

            @pl.when((chunk >= 0) & (chunk < NC))
            def _():
                at = 2 * (step - 1)
                multiply(chunk, lax.rem(z + 4 - step, NZ), keep(at))
                multiply(chunk, lax.rem(z + NZ - 4 + step, NZ), keep(at + 1))
                right_copy(step - 1, chunk).wait_recv()
                if step == 1:
                    right_in[0, chunk, :H] = (own[at, chunk, :H] + right_in[0, chunk, :H].astype(F32)).astype(BF16)
                    right_in[0, chunk, H:] = own[at, chunk, H:].astype(BF16)
                else:
                    right_in[step - 1, chunk] = (own[at, chunk] + right_in[step - 1, chunk].astype(F32)).astype(BF16)
                right_copy(step, chunk).start()
                left_copy(step - 1, chunk).wait_recv()
                if step == 1:
                    left_in[0, chunk, :H] = own[at + 1, chunk, :H].astype(BF16)
                    left_in[0, chunk, H:] = (own[at + 1, chunk, H:] + left_in[0, chunk, H:].astype(F32)).astype(BF16)
                else:
                    left_in[step - 1, chunk] = (own[at + 1, chunk] + left_in[step - 1, chunk].astype(F32)).astype(BF16)
                left_copy(step, chunk).start()

        last = t - 4

        @pl.when((last >= 0) & (last < NC))
        def _():
            multiply(last, z, keep(6))
            right_copy(3, last).wait_recv()
            left_copy(3, last).wait_recv()
            value = own[6, last] + right_in[3, last].astype(F32) + left_in[3, last].astype(F32)
            fin_out[pl.ds(last * BPC, BPC)] = value.astype(BF16).reshape(BPC, RB, W)

            @pl.when(last == 0)
            def _():
                own_rows.start()

            for u in range(BPC):
                @pl.when(last * BPC + u > 0)
                def _():
                    fin_copy(last * BPC + u).start()

        @pl.when(2 * t < NC - AHEAD)
        def _():
            send_amplitudes(AHEAD + 2 * t)
            send_amplitudes(AHEAD + 2 * t + 1)

    own_rows.wait()

    @pl.loop(1, NB)
    def _(slot):
        amp_copy(slot).wait_send()
        fin_copy(slot).wait()

    @pl.loop(0, NC)
    def _(chunk):
        for step in range(4):
            right_copy(step, chunk).wait_send()
            left_copy(step, chunk).wait_send()


def place(q_owner, rows, out, spread):
    for q in range(NB):
        block = rows[q_owner[q]].astype(F32)
        for i in range(PW // 128):
            spread[i, pl.ds(q, RB, stride=STRIDE), :] = block[:, i * 128 : (i + 1) * 128]
    for i in range(PW // 128):
        out[:, :, i * 128 : (i + 1) * 128] = spread[i].reshape(RB, STRIDE, 128)[:, :NB].astype(BF16)


def on_device(amplitudes, amp_tiles, integrals, cd_tiles, q_owner):
    any_space = pl.BlockSpec(memory_space=pl.ANY)
    smem = pl.BlockSpec(memory_space=pltpu.SMEM)
    dma = pltpu.SemaphoreType.DMA
    result = pl.pallas_call(
        kernel,
        out_shape=jax.ShapeDtypeStruct((NB, RB, W), BF16),
        in_specs=[any_space] * 5,
        out_specs=any_space,
        scratch_shapes=[
            pltpu.SMEM((TW, NB), I32),
            pltpu.SMEM((KV, NB), I32),
            pltpu.SMEM((NB,), I32),
            pltpu.VMEM((RB * TW, W), BF16),
            pltpu.VMEM((KV, NZ, W, W), BF16),
            pltpu.VMEM((KV, NB, 128), I32),
            pltpu.VMEM((8, 128), I32),
            pltpu.VMEM((NB, KV, RB, W), BF16),
            pltpu.VMEM((NB, KV, RB, W), BF16),
            pltpu.VMEM((NC, R, W), BF16),
            pltpu.VMEM((7, NC, R, W), F32),
            pltpu.VMEM((4, NC, R, W), BF16),
            pltpu.VMEM((4, NC, R, W), BF16),
            pltpu.VMEM((NB, RB, W), BF16),
            dma((5,)), dma((NZ,)), dma((NB,)), dma((NB,)),
            dma((4, NC)), dma((4, NC)), dma((4, NC)), dma((4, NC)),
            dma((NB,)), dma((NB,)),
        ],
        compiler_params=pltpu.CompilerParams(
            collective_id=0, has_side_effects=True, vmem_limit_bytes=56 * 1024 * 1024),
        name="ladder",
    )(amp_tiles.T, cd_tiles.T, q_owner, amplitudes.reshape(RB * TW, W), integrals.reshape(KV, NZ, W, W))
    return pl.pallas_call(
        place,
        out_shape=jax.ShapeDtypeStruct((RB, NB, W), BF16),
        grid=(W // PW,),
        in_specs=[smem, pl.BlockSpec((NB, RB, PW), lambda i: (0, 0, i))],
        out_specs=pl.BlockSpec((RB, NB, PW), lambda i: (0, 0, i)),
        scratch_shapes=[pltpu.VMEM((PW // 128, RB * STRIDE, 128), F32)],
        name="place",
    )(q_owner, result)


def solution(mesh):
    placed = (P("wide", None, "narrow"), P(), P("wide", None, None, "narrow"), P(), P())
    return jax.shard_map(
        on_device, mesh=mesh, in_specs=placed, out_specs=P("wide", None, "narrow"), check_vma=False
    )
```

```python
import functools

import jax
import jax.numpy as jnp
from jax import lax
from jax.experimental import pallas as pl
from jax.experimental.pallas import tpu as pltpu
from jax.sharding import PartitionSpec as P

MESH = pl.DeviceIdType.MESH
F32, BF16, I32 = jnp.float32, jnp.bfloat16, jnp.int32

NB = 32
RB = 32
TW = 16
KV = 2
NZ = 8
W = 512
BPC = 2
NC = NB // BPC
R = BPC * RB
H = R // 2
PW = 256
STRIDE = 40
SX, SY = 4, 4
AHEAD = 4
SINGLE = 2
CHIPS = [(0, 0), (0, 1), (0, 3), (1, 0), (1, 1), (3, 3), (1, 3), (3, 1), (0, 2), (2, 0), (2, 1), (2, 3), (1, 2), (3, 2), (2, 2), (3, 0)]


def digits(values):
    code = sum(v << (2 * i) for i, v in enumerate(values))
    return code - (1 << 32) if code >= 1 << 31 else code


DY, DX = digits([c[0] for c in CHIPS]), digits([c[1] for c in CHIPS])


def offset(slot):
    chip = slot // 2
    if isinstance(slot, int):
        return (*CHIPS[chip], slot % 2)
    at = 2 * chip
    return lax.shift_right_logical(jnp.int32(DY), at) & 3, lax.shift_right_logical(jnp.int32(DX), at) & 3, slot % 2


def shifted(y, x, core, slot, sign):
    dy, dx, dc = offset(slot)
    if sign < 0:
        dy, dx = SY - dy, SX - dx
    return (lax.rem(y + dy, SY) * SX + lax.rem(x + dx, SX)) * 2 + lax.rem(core + dc, 2)


def dot(a, b):
    return lax.dot_general(a, b, (((1,), (0,)), ((), ())), preferred_element_type=F32)


def dot_t(a, b):
    return lax.dot_general(a, b, (((1,), (1,)), ((), ())), preferred_element_type=F32)


def kernel(
    tiles_hbm, cd_hbm, owner_hbm, amp_hbm, ints_hbm, out,
    amp_tiles, cd_tiles, q_owner,
    amp, ints, wanted, tile_lanes, amp_out, amp_in, first, own, right_in, left_in, fin_out,
    load_sem, ints_sem, amp_send, amp_recv, right_send, right_recv, left_send, left_recv, fin_send, fin_recv,
):
    me = lax.axis_index("wide")
    z = lax.axis_index("narrow")
    core, x, y = lax.rem(me, 2), lax.rem(me // 2, SX), me // (2 * SX)
    z_right, z_left = lax.rem(z + 1, NZ), lax.rem(z + NZ - 1, NZ)

    def ints_copy(part):
        return pltpu.make_async_copy(ints_hbm.at[:, part], ints.at[:, part], ints_sem.at[part])

    load_amp = pltpu.make_async_copy(amp_hbm, amp, load_sem.at[0])
    load_tables = [
        pltpu.make_async_copy(src, dst, load_sem.at[2 + i])
        for i, (src, dst) in enumerate(((tiles_hbm, amp_tiles), (cd_hbm, cd_tiles), (owner_hbm, q_owner)))
    ]
    for load in load_tables:
        load.start()
    load_amp.start()
    ints_copy(lax.rem(z + 4, NZ)).start()

    barrier = pltpu.get_barrier_semaphore()
    for slot in range(1, NB):
        pl.semaphore_signal(barrier, inc=1, device_id=(shifted(y, x, core, slot, 1), z), device_id_type=MESH)
    for there in (z_right, z_left):
        pl.semaphore_signal(barrier, inc=1, device_id=(me, there), device_id_type=MESH)

    for load in load_tables:
        load.wait()
    rows = lax.broadcasted_iota(I32, (NB, 128), 0)
    lanes = lax.broadcasted_iota(I32, (1, 128), 1)
    wants = [jnp.zeros((NB, 128), I32) for _ in range(KV)]
    for q in range(NB):
        owner = q_owner[q]
        for k in range(KV):
            wants[k] = jnp.where(rows == owner, cd_tiles[k, q], wants[k])
    for k in range(KV):
        wanted[k] = wants[k]
    held = jnp.zeros((1, 128), I32)
    for t in range(TW):
        held = jnp.where(lax.rem(lanes, TW) == t, amp_tiles[t, me], held)
    tile_lanes[...] = jnp.broadcast_to(held, (8, 128))

    def amp_copy(slot):
        return pltpu.make_async_remote_copy(
            src_ref=amp_out.at[slot], dst_ref=amp_in.at[slot], send_sem=amp_send.at[slot], recv_sem=amp_recv.at[slot],
            device_id=(shifted(y, x, core, slot, 1), z), device_id_type=MESH)

    def fin_copy(slot):
        return pltpu.make_async_remote_copy(
            src_ref=fin_out.at[slot], dst_ref=out.at[me], send_sem=fin_send.at[slot], recv_sem=fin_recv.at[slot],
            device_id=(shifted(y, x, core, slot, -1), z), device_id_type=MESH)

    def right_copy(step, chunk):
        if step == 0:
            src, dst = first.at[chunk, pl.ds(0, H)], right_in.at[0, chunk, pl.ds(0, H)]
        else:
            src, dst = right_in.at[step - 1, chunk], right_in.at[step, chunk]
        return pltpu.make_async_remote_copy(
            src_ref=src, dst_ref=dst, send_sem=right_send.at[step, chunk], recv_sem=right_recv.at[step, chunk],
            device_id=(me, z_right), device_id_type=MESH)

    def left_copy(step, chunk):
        if step == 0:
            src, dst = first.at[chunk, pl.ds(H, H)], left_in.at[0, chunk, pl.ds(H, H)]
        else:
            src, dst = left_in.at[step - 1, chunk], left_in.at[step, chunk]
        return pltpu.make_async_remote_copy(
            src_ref=src, dst_ref=dst, send_sem=left_send.at[step, chunk], recv_sem=left_recv.at[step, chunk],
            device_id=(me, z_left), device_id_type=MESH)

    for distance in (3, 5, 2, 6, 1, 7, 0):
        ints_copy(lax.rem(z + distance, NZ)).start()

    own_rows = pltpu.make_async_copy(fin_out.at[0], out.at[me], load_sem.at[1])
    load_amp.wait()

    spread_rows = lax.broadcasted_iota(I32, (RB, RB * TW), 0)
    spread_lanes = lax.broadcasted_iota(I32, (RB, RB * TW), 1)
    spread = jnp.where(spread_lanes // TW == spread_rows, 1.0, 0.0)

    def pick_amplitudes(chunk):
        pieces = []
        for u in range(BPC):
            there = shifted(y, x, core, chunk * BPC + u, 1)
            for k in range(KV):
                hit = jnp.where(tile_lanes[pl.ds(0, 1), :] == wanted[k, pl.ds(there, 1), :], 1.0, 0.0)
                hit = jnp.concatenate([hit] * (RB * TW // 128), axis=1)
                pieces.append((spread * hit).astype(BF16))
        picked = dot(jnp.concatenate(pieces, axis=0), amp[...]).astype(BF16)
        amp_out[pl.ds(chunk * BPC, BPC)] = picked.reshape(BPC, KV, RB, W)

        @pl.when(chunk == 0)
        def _():
            amp_in[0] = picked[: KV * RB].reshape(KV, RB, W)

    def send_amplitudes(chunk):
        for u in range(BPC):
            @pl.when(chunk * BPC + u > 0)
            def _():
                amp_copy(chunk * BPC + u).start()

    @pl.loop(0, AHEAD)
    def _(chunk):
        pick_amplitudes(chunk)

    pl.semaphore_wait(barrier, NB - 1 + 2)

    @pl.loop(0, AHEAD)
    def _(chunk):
        send_amplitudes(chunk)

    def multiply(chunk, part, store):
        def go(amount):
            total = None
            for k in range(KV):
                left = amp_in[pl.ds(chunk * BPC, amount * BPC), k].reshape(amount * R, W)
                value = dot_t(left, ints[k, part])
                total = value if total is None else total + value
            store(pl.ds(chunk, amount), total.reshape(amount, R, W))

        @pl.when(chunk == 0)
        def _():
            ints_copy(part).wait()

        @pl.when(chunk < SINGLE)
        def _():
            go(1)

        @pl.when((chunk >= SINGLE) & (chunk % 2 == 0))
        def _():
            go(2)

    def keep(index):
        def store(span, value):
            own[index, span] = value

        return store

    def keep_first(span, value):
        first[span] = value.astype(BF16)

    def arrived(chunk):
        for u in range(BPC):
            @pl.when(chunk * BPC + u > 0)
            def _():
                amp_copy(chunk * BPC + u).wait_recv()

    @pl.loop(0, NC + 4)
    def _(t):
        @pl.when(t < NC)
        def _():
            @pl.when((t < SINGLE) | (t % 2 == 0))
            def _():
                arrived(t)

            @pl.when((t >= SINGLE) & (t % 2 == 0))
            def _():
                arrived(t + 1)

            multiply(t, lax.rem(z + 4, NZ), keep_first)
            right_copy(0, t).start()
            left_copy(0, t).start()

        for step in (1, 2, 3):
            chunk = t - step

            @pl.when((chunk >= 0) & (chunk < NC))
            def _():
                at = 2 * (step - 1)
                multiply(chunk, lax.rem(z + 4 - step, NZ), keep(at))
                multiply(chunk, lax.rem(z + NZ - 4 + step, NZ), keep(at + 1))
                right_copy(step - 1, chunk).wait_recv()
                if step == 1:
                    right_in[0, chunk, :H] = (own[at, chunk, :H] + right_in[0, chunk, :H].astype(F32)).astype(BF16)
                    right_in[0, chunk, H:] = own[at, chunk, H:].astype(BF16)
                else:
                    right_in[step - 1, chunk] = (own[at, chunk] + right_in[step - 1, chunk].astype(F32)).astype(BF16)
                right_copy(step, chunk).start()
                left_copy(step - 1, chunk).wait_recv()
                if step == 1:
                    left_in[0, chunk, :H] = own[at + 1, chunk, :H].astype(BF16)
                    left_in[0, chunk, H:] = (own[at + 1, chunk, H:] + left_in[0, chunk, H:].astype(F32)).astype(BF16)
                else:
                    left_in[step - 1, chunk] = (own[at + 1, chunk] + left_in[step - 1, chunk].astype(F32)).astype(BF16)
                left_copy(step, chunk).start()

        last = t - 4

        @pl.when((last >= 0) & (last < NC))
        def _():
            multiply(last, z, keep(6))
            right_copy(3, last).wait_recv()
            left_copy(3, last).wait_recv()
            value = own[6, last] + right_in[3, last].astype(F32) + left_in[3, last].astype(F32)
            fin_out[pl.ds(last * BPC, BPC)] = value.astype(BF16).reshape(BPC, RB, W)

            @pl.when(last == 0)
            def _():
                own_rows.start()

            for u in range(BPC):
                @pl.when(last * BPC + u > 0)
                def _():
                    fin_copy(last * BPC + u).start()

        @pl.when(2 * t < NC - AHEAD)
        def _():
            for more in range(2):
                pick_amplitudes(AHEAD + 2 * t + more)
                send_amplitudes(AHEAD + 2 * t + more)

    own_rows.wait()

    @pl.loop(1, NB)
    def _(slot):
        amp_copy(slot).wait_send()
        fin_copy(slot).wait()

    @pl.loop(0, NC)
    def _(chunk):
        for step in range(4):
            right_copy(step, chunk).wait_send()
            left_copy(step, chunk).wait_send()


def place(q_owner, rows, out, spread):
    for q in range(NB):
        block = rows[q_owner[q]].astype(F32)
        for i in range(PW // 128):
            spread[i, pl.ds(q, RB, stride=STRIDE), :] = block[:, i * 128 : (i + 1) * 128]
    for i in range(PW // 128):
        out[:, :, i * 128 : (i + 1) * 128] = spread[i].reshape(RB, STRIDE, 128)[:, :NB].astype(BF16)


def on_device(amplitudes, amp_tiles, integrals, cd_tiles, q_owner):
    any_space = pl.BlockSpec(memory_space=pl.ANY)
    smem = pl.BlockSpec(memory_space=pltpu.SMEM)
    dma = pltpu.SemaphoreType.DMA
    result = pl.pallas_call(
        kernel,
        out_shape=jax.ShapeDtypeStruct((NB, RB, W), BF16),
        in_specs=[any_space] * 5,
        out_specs=any_space,
        scratch_shapes=[
            pltpu.SMEM((TW, NB), I32),
            pltpu.SMEM((KV, NB), I32),
            pltpu.SMEM((NB,), I32),
            pltpu.VMEM((RB * TW, W), BF16),
            pltpu.VMEM((KV, NZ, W, W), BF16),
            pltpu.VMEM((KV, NB, 128), I32),
            pltpu.VMEM((8, 128), I32),
            pltpu.VMEM((NB, KV, RB, W), BF16),
            pltpu.VMEM((NB, KV, RB, W), BF16),
            pltpu.VMEM((NC, R, W), BF16),
            pltpu.VMEM((7, NC, R, W), F32),
            pltpu.VMEM((4, NC, R, W), BF16),
            pltpu.VMEM((4, NC, R, W), BF16),
            pltpu.VMEM((NB, RB, W), BF16),
            dma((5,)), dma((NZ,)), dma((NB,)), dma((NB,)),
            dma((4, NC)), dma((4, NC)), dma((4, NC)), dma((4, NC)),
            dma((NB,)), dma((NB,)),
        ],
        compiler_params=pltpu.CompilerParams(
            collective_id=0, has_side_effects=True, vmem_limit_bytes=56 * 1024 * 1024),
        name="ladder",
    )(amp_tiles.T, cd_tiles.T, q_owner, amplitudes.reshape(RB * TW, W), integrals.reshape(KV, NZ, W, W))
    return pl.pallas_call(
        place,
        out_shape=jax.ShapeDtypeStruct((RB, NB, W), BF16),
        grid=(W // PW,),
        in_specs=[smem, pl.BlockSpec((NB, RB, PW), lambda i: (0, 0, i))],
        out_specs=pl.BlockSpec((RB, NB, PW), lambda i: (0, 0, i)),
        scratch_shapes=[pltpu.VMEM((PW // 128, RB * STRIDE, 128), F32)],
        name="place",
    )(q_owner, result)


def solution(mesh):
    placed = (P("wide", None, "narrow"), P(), P("wide", None, None, "narrow"), P(), P())
    return jax.shard_map(
        on_device, mesh=mesh, in_specs=placed, out_specs=P("wide", None, "narrow"), check_vma=False
    )
```

```python
import functools

import jax
import jax.numpy as jnp
from jax import lax
from jax.experimental import pallas as pl
from jax.experimental.pallas import tpu as pltpu
from jax.sharding import PartitionSpec as P

MESH = pl.DeviceIdType.MESH
F32, BF16, I32 = jnp.float32, jnp.bfloat16, jnp.int32

NB = 32
RB = 32
TW = 16
KV = 2
NZ = 8
W = 512
BPC = 2
NC = NB // BPC
R = BPC * RB
H = R // 2
PW = 256
STRIDE = 40
SX, SY = 4, 4
AHEAD = 6
SINGLE = 2
CHIPS = [(0, 0), (0, 1), (0, 3), (1, 0), (1, 1), (3, 3), (1, 3), (3, 1), (0, 2), (2, 0), (2, 1), (2, 3), (1, 2), (3, 2), (2, 2), (3, 0)]


def digits(values):
    code = sum(v << (2 * i) for i, v in enumerate(values))
    return code - (1 << 32) if code >= 1 << 31 else code


DY, DX = digits([c[0] for c in CHIPS]), digits([c[1] for c in CHIPS])


def offset(slot):
    chip = slot // 2
    if isinstance(slot, int):
        return (*CHIPS[chip], slot % 2)
    at = 2 * chip
    return lax.shift_right_logical(jnp.int32(DY), at) & 3, lax.shift_right_logical(jnp.int32(DX), at) & 3, slot % 2


def shifted(y, x, core, slot, sign):
    dy, dx, dc = offset(slot)
    if sign < 0:
        dy, dx = SY - dy, SX - dx
    return (lax.rem(y + dy, SY) * SX + lax.rem(x + dx, SX)) * 2 + lax.rem(core + dc, 2)


def dot(a, b):
    return lax.dot_general(a, b, (((1,), (0,)), ((), ())), preferred_element_type=F32)


def dot_t(a, b):
    return lax.dot_general(a, b, (((1,), (1,)), ((), ())), preferred_element_type=F32)


def kernel(
    tiles_hbm, cd_hbm, owner_hbm, amp_hbm, ints_hbm, out,
    amp_tiles, cd_tiles, q_owner,
    amp, ints, wanted, tile_lanes, amp_out, amp_in, first, own, right_in, left_in, fin_out,
    load_sem, ints_sem, amp_send, amp_recv, right_send, right_recv, left_send, left_recv, fin_send, fin_recv,
):
    me = lax.axis_index("wide")
    z = lax.axis_index("narrow")
    core, x, y = lax.rem(me, 2), lax.rem(me // 2, SX), me // (2 * SX)
    z_right, z_left = lax.rem(z + 1, NZ), lax.rem(z + NZ - 1, NZ)

    def ints_copy(part):
        return pltpu.make_async_copy(ints_hbm.at[:, part], ints.at[:, part], ints_sem.at[part])

    load_amp = pltpu.make_async_copy(amp_hbm, amp, load_sem.at[0])
    load_tables = [
        pltpu.make_async_copy(src, dst, load_sem.at[2 + i])
        for i, (src, dst) in enumerate(((tiles_hbm, amp_tiles), (cd_hbm, cd_tiles), (owner_hbm, q_owner)))
    ]
    for load in load_tables:
        load.start()
    load_amp.start()
    ints_copy(lax.rem(z + 4, NZ)).start()

    barrier = pltpu.get_barrier_semaphore()
    for slot in range(1, NB):
        pl.semaphore_signal(barrier, inc=1, device_id=(shifted(y, x, core, slot, 1), z), device_id_type=MESH)
    for there in (z_right, z_left):
        pl.semaphore_signal(barrier, inc=1, device_id=(me, there), device_id_type=MESH)

    for load in load_tables:
        load.wait()
    rows = lax.broadcasted_iota(I32, (NB, 128), 0)
    lanes = lax.broadcasted_iota(I32, (1, 128), 1)
    wants = [jnp.zeros((NB, 128), I32) for _ in range(KV)]
    for q in range(NB):
        owner = q_owner[q]
        for k in range(KV):
            wants[k] = jnp.where(rows == owner, cd_tiles[k, q], wants[k])
    for k in range(KV):
        wanted[k] = wants[k]
    held = jnp.zeros((1, 128), I32)
    for t in range(TW):
        held = jnp.where(lax.rem(lanes, TW) == t, amp_tiles[t, me], held)
    tile_lanes[...] = jnp.broadcast_to(held, (8, 128))

    def amp_copy(slot):
        return pltpu.make_async_remote_copy(
            src_ref=amp_out.at[slot], dst_ref=amp_in.at[slot], send_sem=amp_send.at[slot], recv_sem=amp_recv.at[slot],
            device_id=(shifted(y, x, core, slot, 1), z), device_id_type=MESH)

    def fin_copy(slot):
        return pltpu.make_async_remote_copy(
            src_ref=fin_out.at[slot], dst_ref=out.at[me], send_sem=fin_send.at[slot], recv_sem=fin_recv.at[slot],
            device_id=(shifted(y, x, core, slot, -1), z), device_id_type=MESH)

    def right_copy(step, chunk):
        if step == 0:
            src, dst = first.at[chunk, pl.ds(0, H)], right_in.at[0, chunk, pl.ds(0, H)]
        else:
            src, dst = right_in.at[step - 1, chunk], right_in.at[step, chunk]
        return pltpu.make_async_remote_copy(
            src_ref=src, dst_ref=dst, send_sem=right_send.at[step, chunk], recv_sem=right_recv.at[step, chunk],
            device_id=(me, z_right), device_id_type=MESH)

    def left_copy(step, chunk):
        if step == 0:
            src, dst = first.at[chunk, pl.ds(H, H)], left_in.at[0, chunk, pl.ds(H, H)]
        else:
            src, dst = left_in.at[step - 1, chunk], left_in.at[step, chunk]
        return pltpu.make_async_remote_copy(
            src_ref=src, dst_ref=dst, send_sem=left_send.at[step, chunk], recv_sem=left_recv.at[step, chunk],
            device_id=(me, z_left), device_id_type=MESH)

    for distance in (3, 5, 2, 6, 1, 7, 0):
        ints_copy(lax.rem(z + distance, NZ)).start()

    own_rows = pltpu.make_async_copy(fin_out.at[0], out.at[me], load_sem.at[1])
    load_amp.wait()

    spread_rows = lax.broadcasted_iota(I32, (RB, RB * TW), 0)
    spread_lanes = lax.broadcasted_iota(I32, (RB, RB * TW), 1)
    spread = jnp.where(spread_lanes // TW == spread_rows, 1.0, 0.0)

    def pick_amplitudes(chunk):
        pieces = []
        for u in range(BPC):
            there = shifted(y, x, core, chunk * BPC + u, 1)
            for k in range(KV):
                hit = jnp.where(tile_lanes[pl.ds(0, 1), :] == wanted[k, pl.ds(there, 1), :], 1.0, 0.0)
                hit = jnp.concatenate([hit] * (RB * TW // 128), axis=1)
                pieces.append((spread * hit).astype(BF16))
        picked = dot(jnp.concatenate(pieces, axis=0), amp[...]).astype(BF16)
        amp_out[pl.ds(chunk * BPC, BPC)] = picked.reshape(BPC, KV, RB, W)

        @pl.when(chunk == 0)
        def _():
            amp_in[0] = picked[: KV * RB].reshape(KV, RB, W)

    def send_amplitudes(chunk):
        for u in range(BPC):
            @pl.when(chunk * BPC + u > 0)
            def _():
                amp_copy(chunk * BPC + u).start()

    @pl.loop(0, AHEAD)
    def _(chunk):
        pick_amplitudes(chunk)

    pl.semaphore_wait(barrier, NB - 1 + 2)

    @pl.loop(0, AHEAD)
    def _(chunk):
        send_amplitudes(chunk)

    def multiply(chunk, part, store):
        def go(amount):
            total = None
            for k in range(KV):
                left = amp_in[pl.ds(chunk * BPC, amount * BPC), k].reshape(amount * R, W)
                value = dot_t(left, ints[k, part])
                total = value if total is None else total + value
            store(pl.ds(chunk, amount), total.reshape(amount, R, W))

        @pl.when(chunk == 0)
        def _():
            ints_copy(part).wait()

        @pl.when(chunk < SINGLE)
        def _():
            go(1)

        @pl.when((chunk >= SINGLE) & (chunk % 2 == 0))
        def _():
            go(2)

    def keep(index):
        def store(span, value):
            own[index, span] = value

        return store

    def keep_first(span, value):
        first[span] = value.astype(BF16)

    def arrived(chunk):
        for u in range(BPC):
            @pl.when(chunk * BPC + u > 0)
            def _():
                amp_copy(chunk * BPC + u).wait_recv()

    @pl.loop(0, NC + 4)
    def _(t):
        @pl.when(t < NC)
        def _():
            @pl.when((t < SINGLE) | (t % 2 == 0))
            def _():
                arrived(t)

            @pl.when((t >= SINGLE) & (t % 2 == 0))
            def _():
                arrived(t + 1)

            multiply(t, lax.rem(z + 4, NZ), keep_first)
            right_copy(0, t).start()
            left_copy(0, t).start()

        for step in (1, 2, 3):
            chunk = t - step

            @pl.when((chunk >= 0) & (chunk < NC))
            def _():
                at = 2 * (step - 1)
                multiply(chunk, lax.rem(z + 4 - step, NZ), keep(at))
                multiply(chunk, lax.rem(z + NZ - 4 + step, NZ), keep(at + 1))
                right_copy(step - 1, chunk).wait_recv()
                if step == 1:
                    right_in[0, chunk, :H] = (own[at, chunk, :H] + right_in[0, chunk, :H].astype(F32)).astype(BF16)
                    right_in[0, chunk, H:] = own[at, chunk, H:].astype(BF16)
                else:
                    right_in[step - 1, chunk] = (own[at, chunk] + right_in[step - 1, chunk].astype(F32)).astype(BF16)
                right_copy(step, chunk).start()
                left_copy(step - 1, chunk).wait_recv()
                if step == 1:
                    left_in[0, chunk, :H] = own[at + 1, chunk, :H].astype(BF16)
                    left_in[0, chunk, H:] = (own[at + 1, chunk, H:] + left_in[0, chunk, H:].astype(F32)).astype(BF16)
                else:
                    left_in[step - 1, chunk] = (own[at + 1, chunk] + left_in[step - 1, chunk].astype(F32)).astype(BF16)
                left_copy(step, chunk).start()

        last = t - 4

        @pl.when((last >= 0) & (last < NC))
        def _():
            multiply(last, z, keep(6))
            right_copy(3, last).wait_recv()
            left_copy(3, last).wait_recv()
            value = own[6, last] + right_in[3, last].astype(F32) + left_in[3, last].astype(F32)
            fin_out[pl.ds(last * BPC, BPC)] = value.astype(BF16).reshape(BPC, RB, W)

            @pl.when(last == 0)
            def _():
                own_rows.start()

            for u in range(BPC):
                @pl.when(last * BPC + u > 0)
                def _():
                    fin_copy(last * BPC + u).start()

        @pl.when(2 * t < NC - AHEAD)
        def _():
            for more in range(2):
                pick_amplitudes(AHEAD + 2 * t + more)
                send_amplitudes(AHEAD + 2 * t + more)

    own_rows.wait()

    @pl.loop(1, NB)
    def _(slot):
        amp_copy(slot).wait_send()
        fin_copy(slot).wait()

    @pl.loop(0, NC)
    def _(chunk):
        for step in range(4):
            right_copy(step, chunk).wait_send()
            left_copy(step, chunk).wait_send()


def place(q_owner, rows, out, spread):
    for q in range(NB):
        block = rows[q_owner[q]].astype(F32)
        for i in range(PW // 128):
            spread[i, pl.ds(q, RB, stride=STRIDE), :] = block[:, i * 128 : (i + 1) * 128]
    for i in range(PW // 128):
        out[:, :, i * 128 : (i + 1) * 128] = spread[i].reshape(RB, STRIDE, 128)[:, :NB].astype(BF16)


def on_device(amplitudes, amp_tiles, integrals, cd_tiles, q_owner):
    any_space = pl.BlockSpec(memory_space=pl.ANY)
    smem = pl.BlockSpec(memory_space=pltpu.SMEM)
    dma = pltpu.SemaphoreType.DMA
    result = pl.pallas_call(
        kernel,
        out_shape=jax.ShapeDtypeStruct((NB, RB, W), BF16),
        in_specs=[any_space] * 5,
        out_specs=any_space,
        scratch_shapes=[
            pltpu.SMEM((TW, NB), I32),
            pltpu.SMEM((KV, NB), I32),
            pltpu.SMEM((NB,), I32),
            pltpu.VMEM((RB * TW, W), BF16),
            pltpu.VMEM((KV, NZ, W, W), BF16),
            pltpu.VMEM((KV, NB, 128), I32),
            pltpu.VMEM((8, 128), I32),
            pltpu.VMEM((NB, KV, RB, W), BF16),
            pltpu.VMEM((NB, KV, RB, W), BF16),
            pltpu.VMEM((NC, R, W), BF16),
            pltpu.VMEM((7, NC, R, W), F32),
            pltpu.VMEM((4, NC, R, W), BF16),
            pltpu.VMEM((4, NC, R, W), BF16),
            pltpu.VMEM((NB, RB, W), BF16),
            dma((5,)), dma((NZ,)), dma((NB,)), dma((NB,)),
            dma((4, NC)), dma((4, NC)), dma((4, NC)), dma((4, NC)),
            dma((NB,)), dma((NB,)),
        ],
        compiler_params=pltpu.CompilerParams(
            collective_id=0, has_side_effects=True, vmem_limit_bytes=56 * 1024 * 1024),
        name="ladder",
    )(amp_tiles.T, cd_tiles.T, q_owner, amplitudes.reshape(RB * TW, W), integrals.reshape(KV, NZ, W, W))
    return pl.pallas_call(
        place,
        out_shape=jax.ShapeDtypeStruct((RB, NB, W), BF16),
        grid=(W // PW,),
        in_specs=[smem, pl.BlockSpec((NB, RB, PW), lambda i: (0, 0, i))],
        out_specs=pl.BlockSpec((RB, NB, PW), lambda i: (0, 0, i)),
        scratch_shapes=[pltpu.VMEM((PW // 128, RB * STRIDE, 128), F32)],
        name="place",
    )(q_owner, result)


def solution(mesh):
    placed = (P("wide", None, "narrow"), P(), P("wide", None, None, "narrow"), P(), P())
    return jax.shard_map(
        on_device, mesh=mesh, in_specs=placed, out_specs=P("wide", None, "narrow"), check_vma=False
    )
```
